32 devices in a mesh: dp: 8 (over z, core), tp: 4 (over y, x).
Axes of the slice: x: 2, y: 2, z: 4, core: 2. Of those that a mesh axis runs over, the one named last changes fastest.
Arguments:
- partials: bfloat16 [4, 1280, 7680], P('tp', 'dp'), may hold values from -1.5 to 1.5
- layer_input: bfloat16 [1920, 1280], P(('dp', 'tp')), may hold values from -6 to 6
- ln_gain: float32 [1280], replicated, may hold values from 0.25 to 1.75
- ln_bias: float32 [1280], replicated, may hold values from -3 to 3
- fc1_weight: bfloat16 [1280, 5120], P(None, 'tp'), may hold values from -0.15625 to 0.15625
- fc1_bias: float32 [5120], P('tp'), may hold values from -3 to 3
- fc2_weight: bfloat16 [1280, 5120], P(None, 'tp'), may hold values from -0.078125 to 0.078125
- row_rank: int32 [1280, 1], P('dp'), may hold values from 0 to 3; in each aligned block of 160 rows (0 to 159, 160 to 319, ...) at most 60 rows name the same one
Outputs:
- early_grads: bfloat16 [1920, 6400], P(('dp', 'tp'))
- fc1_grad: bfloat16 [1280, 5120], P('dp', 'tp')
- fc2_grad: bfloat16 [1280, 5120], P('dp', 'tp')
The draws below stay inside these ranges and needn't reach their ends.
Inputs may be any that keep to these rules, and one draw needn't show every extreme that they name: `row_rank`: in each aligned block of 160 rows (one data replica) no rank is named by more than 60 rows, a bound that some block reaches.
All inputs are finite; a program needn't handle non-finite values.
Results may differ from the reference program's by a relative error of at most 0.029.
Values may be sent and summed in bfloat16 or wider, within the bound.
A program may use at most 64 MiB of HBM per device.

```python
import math
import jax
import jax.numpy as jnp
import numpy as np
from jax import lax

D = 1280
HID = 5120
VIS = 7680
ROWS = 160
MOST = 60
TOTAL_ROWS = 1280
SLOTS = 1920
N_DP = 8
N_TP = 4


def level_of(stream_key, shape, shards, smallest, high):
    loudness, own = 1.0, jax.random.fold_in(stream_key, 6)
    for axis_at, parts in shards:
        steps = jnp.exp(jax.random.uniform(jax.random.fold_in(own, axis_at), (parts,), jnp.float32, smallest / len(shards), high / len(shards)))
        loudness = loudness * jnp.repeat(steps, shape[axis_at] // parts).reshape([-1 if axis == axis_at else 1 for axis in range(len(shape))])
    return loudness


def routed_block(own_key, own, number, rows, amount, top, most, lean):
    ranking = jax.random.permutation(own_key, amount)
    packed, usual = shares(amount, rows * top, most, lean, True), shares(amount, rows * top, most, lean, False)
    places = jnp.arange(amount)

    def named(tallies, rotation):
        used = int((tallies > 0).sum())
        fixed = max(1, used // 4)
        moved = fixed + (places - fixed + rotation * (used - fixed)) % max(1, amount - fixed)
        return jnp.zeros((amount,), jnp.int32).at[ranking[jnp.where(places < fixed, places, moved)]].set(jnp.asarray(tallies, jnp.int32))

    tallies = jnp.where(number % 4 == 0, named(packed, number // 4), named(usual, number - number // 4 - 1))
    mixed = jax.random.permutation(jax.random.fold_in(own, 3), amount)
    giver, sink = mixed[0:amount // 2 * 2:2], mixed[1:amount // 2 * 2:2]
    room = jnp.minimum(tallies[giver] - 1, most - tallies[sink]) // 2
    room = jnp.where((giver == ranking[0]) | (sink == ranking[0]) | (tallies[sink] == 0), 0, jnp.maximum(room, 0))
    moved = jax.random.randint(jax.random.fold_in(own, 4), (amount // 2,), 0, 1 << 20) % (room + 1)
    tallies = tallies.at[giver].add(-moved).at[sink].add(moved)
    members = jnp.searchsorted(jnp.cumsum(tallies), jnp.arange(rows * top), side="right").astype(jnp.int32)
    grid = members.reshape(top, rows).T
    grid = grid[jax.random.permutation(jax.random.fold_in(own, 1), rows)]
    rotation = jax.random.randint(jax.random.fold_in(own, 2), (rows, 1), 0, top)
    return jnp.take_along_axis(grid, (jnp.arange(top)[None, :] + rotation) % top, axis=1)


def shares(amount, total, most, skew, full):
    weights = [(1 << 20) // math.isqrt(standing ** skew) + 1 for standing in range(1, amount + 1)]
    largest = most if full else min(most, max(-(-total // amount), total * weights[0] // sum(weights)))
    least = 1 if total - largest >= amount - 1 else 0
    given, spare = [largest] + [least] * (amount - 1), total - largest - least * (amount - 1)
    while spare > 0:
        candidates = [i for i in range(1, amount) if given[i] < largest] or [i for i in range(1, amount) if given[i] < most]
        pool, left = sum([weights[i] for i in candidates]), spare
        for i in candidates:
            more = min(most - given[i], max(1, left * weights[i] // pool), spare)
            given[i] = given[i] + more
            spare = spare - more
    return np.array(given)


def gaussian(own_key, extent, scale, most, shards=(), kind=jnp.bfloat16):
    gain = level_of(own_key, extent, shards, -0.22, 0.18) if shards else 1.0
    drawn = jax.random.normal(own_key, extent, jnp.float32) * scale * gain
    return jnp.minimum(jnp.maximum(drawn, -most), most).astype(kind)


def setup_inputs(seed: int = 0) -> dict:
    key_of = jax.random.split(jax.random.key(seed), 9)
    partials = gaussian(key_of[0], (N_TP, TOTAL_ROWS, VIS), 0.25, 1.5, ((0, 4), (1, 8)))
    layer_input = gaussian(key_of[1], (SLOTS, D), 1.0, 6.0, ((0, 32),))
    ln_gain = jnp.clip(1.0 + 0.15 * jax.random.normal(key_of[2], (D,), jnp.float32), 0.25, 1.75)
    ln_bias = gaussian(key_of[3], (D,), 0.5, 3.0, (), jnp.float32)
    fc1_weight = gaussian(key_of[4], (D, HID), D ** -0.5, 0.15625, ((1, 4),))
    fc1_bias = gaussian(key_of[5], (HID,), 0.5, 3.0, ((0, 4),), jnp.float32)
    fc2_weight = gaussian(key_of[6], (D, HID), HID ** -0.5, 0.078125, ((1, 4),))
    row_rank_keys = jax.random.split(jax.random.fold_in(key_of[7], 1), TOTAL_ROWS // ROWS)
    row_rank_turns = jax.random.permutation(jax.random.fold_in(key_of[7], 3), TOTAL_ROWS // ROWS)
    row_rank = jax.vmap(lambda own, number: routed_block(jax.random.fold_in(key_of[7], 2), own, number, ROWS, N_TP, 1, MOST, 2))(row_rank_keys, row_rank_turns).reshape((TOTAL_ROWS, 1))
    return dict(partials=partials, layer_input=layer_input, ln_gain=ln_gain, ln_bias=ln_bias, fc1_weight=fc1_weight, fc1_bias=fc1_bias, fc2_weight=fc2_weight, row_rank=row_rank)


def gelu_parts(preact):
    normal_cdf = 0.5 * (1.0 + lax.erf(preact * 0.7071067811865476))
    density = jnp.exp(-0.5 * preact * preact) * 0.3989422804014327
    return (preact * normal_cdf, normal_cdf + preact * density)

def slot_matrix(rank_ids, groups, slot_count):
    columns = jnp.arange(groups, dtype=jnp.int32)
    onehot = (rank_ids[:, None] == columns[None, :]).astype(jnp.int32)
    position = jnp.cumsum(onehot, axis=0) - 1
    own_position = lax.optimization_barrier(jnp.sum(position * onehot, axis=1))
    slot_ids = rank_ids * slot_count + own_position
    targets = jnp.arange(groups * slot_count, dtype=jnp.int32)
    return (targets[:, None] == slot_ids[None, :]).astype(jnp.bfloat16)

def normalize(layer_rows, ln_gain, ln_bias):
    values = layer_rows.astype(jnp.float32)
    row_mean = lax.optimization_barrier(jnp.mean(values, axis=1, keepdims=True))
    centered = values - row_mean
    row_var = lax.optimization_barrier(jnp.mean(centered * centered, axis=1, keepdims=True))
    return (centered / jnp.sqrt(row_var + 1e-05) * ln_gain + ln_bias).astype(jnp.bfloat16)

def reference(partials, layer_input, ln_gain, ln_bias, fc1_weight, fc1_bias, fc2_weight, row_rank):
    factor = float(N_DP * ROWS) ** (-0.5)

    def replica_step(carry, replica):
        first_sum, second_sum = carry
        replica_parts = lax.dynamic_slice_in_dim(partials, replica * ROWS, ROWS, 1)
        summed = lax.optimization_barrier(jnp.sum(replica_parts.astype(jnp.float32), axis=0)).astype(jnp.bfloat16)
        rank_ids = lax.dynamic_slice_in_dim(row_rank[:, 0], replica * ROWS, ROWS, 0).astype(jnp.int32)
        table = slot_matrix(rank_ids, N_TP, MOST)
        placed = jnp.dot(table, summed, preferred_element_type=jnp.float32).astype(jnp.bfloat16)
        layer_rows = lax.dynamic_slice_in_dim(layer_input, replica * N_TP * MOST, N_TP * MOST, 0)
        normed = normalize(layer_rows, ln_gain, ln_bias)
        upstream = placed[:, :D]
        preact = jnp.dot(normed, fc1_weight, preferred_element_type=jnp.float32) + fc1_bias
        activated, derivative = gelu_parts(preact)
        hidden = activated.astype(jnp.bfloat16)
        hidden_grad = jnp.dot(upstream, fc2_weight, preferred_element_type=jnp.float32)
        preact_grad = (hidden_grad * derivative).astype(jnp.bfloat16)
        grad_first = (jnp.dot(normed.T, preact_grad, preferred_element_type=jnp.float32) * factor).astype(jnp.bfloat16)
        grad_second = (jnp.dot(upstream.T, hidden, preferred_element_type=jnp.float32) * factor).astype(jnp.bfloat16)
        carry = (first_sum + grad_first.astype(jnp.float32), second_sum + grad_second.astype(jnp.float32))
        return (carry, placed[:, D:])
    start = (jnp.zeros((D, HID), jnp.float32), jnp.zeros((D, HID), jnp.float32))
    (first_sum, second_sum), early = lax.scan(replica_step, start, jnp.arange(N_DP, dtype=jnp.int32))
    early_grads = early.reshape(N_DP * N_TP * MOST, VIS - D)
    return (early_grads, first_sum.astype(jnp.bfloat16), second_sum.astype(jnp.bfloat16))
```

```python
import functools

import jax
import jax.numpy as jnp
from jax import lax
from jax.experimental import pallas as pl
from jax.experimental.pallas import tpu as pltpu
from jax.sharding import PartitionSpec as P

MESH = pl.DeviceIdType.MESH
CORES = 2
F32 = jnp.float32
BF16 = jnp.bfloat16


def up_to(value, step):
    return -(-value // step) * step


def onehot(rows, columns, wanted, axis):
    at = lax.broadcasted_iota(jnp.int32, (rows, columns), axis).astype(F32)
    return jnp.where(at == wanted, 1.0, 0.0).astype(BF16)


def fdot(left, right):
    return jnp.dot(left, right, preferred_element_type=F32)


def kernel(
    n_tp, n_dp, share, factor,
    rank_row, rank_col, part, lin, gain, bias, fc1, b1, fc2,
    early_o, g1_o, g2_o,
    partu, parte, w1, w2, linall, usend, urecv, uall, esend, erecv,
    hidden, deriv, nts, ntr, upt, terms, cross, chain, grads,
    lsem, tsem, dsem, zsem,
):
    me_tp = lax.axis_index("tp")
    me_dp = lax.axis_index("dp")
    z, core = me_dp // CORES, me_dp % CORES
    nz = n_dp // CORES
    partner = {"dp": z * CORES + 1 - core}
    rows, width = partu.shape
    slot_pad = lin.shape[0]
    share_pad = usend.shape[1]
    hid = w1.shape[1]
    depth = g1_o.shape[0]
    step_h = 256 if hid % 256 == 0 else hid

    loads = [
        pltpu.make_async_copy(part.at[:, pl.ds(0, width)], partu, lsem.at[0]),
        pltpu.make_async_copy(part.at[:, pl.ds(width, parte.shape[1])], parte, lsem.at[1]),
        pltpu.make_async_copy(fc1, w1, lsem.at[2]),
        pltpu.make_async_copy(fc2, w2, lsem.at[3]),
    ]
    for load in loads:
        load.start()

    barrier = pltpu.get_barrier_semaphore()
    for i in range(1, n_tp):
        pl.semaphore_signal(barrier, inc=1, device_id={"tp": (me_tp + i) % n_tp}, device_id_type=MESH)
    for i in range(1, n_dp):
        pl.semaphore_signal(barrier, inc=1, device_id={"dp": (me_dp + i) % n_dp}, device_id_type=MESH)
    pl.semaphore_wait(barrier, n_tp + n_dp - 2)

    def remote(src, dst, send, recv, device):
        return pltpu.make_async_remote_copy(
            src_ref=src, dst_ref=dst, send_sem=send, recv_sem=recv, device_id=device, device_id_type=MESH
        )

    def tp_send(src_of, dst, kind):
        for i in range(1, n_tp):
            to = (me_tp + i) % n_tp
            remote(src_of(to), dst.at[me_tp], tsem.at[kind, to], tsem.at[kind + 1, me_tp], {"tp": to}).start()

    def tp_wait(src_of, dst, kind, recv):
        for i in range(1, n_tp):
            to = (me_tp + i) % n_tp
            copy = remote(src_of(to), dst.at[to], tsem.at[kind, to], tsem.at[kind + 1, to], {"tp": to})
            if recv:
                copy.wait_recv()
            else:
                copy.wait_send()

    own_lin = lambda to: lin
    u_block = lambda to: usend.at[to]
    own_up = lambda to: uall.at[me_tp]
    e_block = lambda to: esend.at[to]

    r_row = lax.broadcasted_iota(jnp.int32, (1, rows), 1)
    r_col = lax.broadcasted_iota(jnp.int32, (rows, 1), 0)
    pad_row, pad_col = (r_row * 0).astype(F32), (r_col * 0).astype(F32)
    for i in range(1, n_tp):
        pad_row = pad_row + jnp.where(r_row >= i * share, 1.0, 0.0)
        pad_col = pad_col + jnp.where(r_col >= i * share, 1.0, 0.0)
    pad_row = r_row.astype(F32) + pad_row * (share_pad - share)
    pad_col = r_col.astype(F32) + pad_col * (share_pad - share)

    loads[0].wait()
    spread = onehot(n_tp * share_pad, rows, pad_row, 0)
    usend[...] = fdot(spread, partu[...]).astype(BF16).reshape(usend.shape)
    tp_send(u_block, urecv, 0)
    tp_send(own_lin, linall, 4)
    linall[me_tp] = lin[...]

    rank_r, rank_c = rank_row[...], rank_col[...]
    same = rank_c == rank_r
    at0 = lax.broadcasted_iota(jnp.int32, (rows, rows), 0)
    at1 = lax.broadcasted_iota(jnp.int32, (rows, rows), 1)
    place_r = jnp.sum(jnp.where(same & (at0 < at1), 1.0, 0.0), axis=0, keepdims=True)
    place_c = jnp.sum(jnp.where(same & (at1 < at0), 1.0, 0.0), axis=1, keepdims=True)
    slot_r = rank_r.astype(F32) * slot_pad + place_r
    slot_c = rank_c.astype(F32) * slot_pad + place_c
    table = onehot(n_tp * slot_pad, rows, slot_r, 0)
    back = onehot(rows, n_tp * slot_pad, slot_c, 1)

    loads[1].wait()

    def place(i, carry):
        columns = pl.ds(pl.multiple_of(i * width, 128), width)
        placed = fdot(table, parte[:, columns]).astype(BF16)
        esend[:, :, columns] = placed.reshape(n_tp, slot_pad, width)
        return carry

    lax.fori_loop(0, parte.shape[1] // width, place, 0)

    tp_wait(u_block, urecv, 0, True)
    total = usend[me_tp].astype(F32)
    for i in range(1, n_tp):
        total = total + urecv[(me_tp + i) % n_tp].astype(F32)
    uall[me_tp] = total.astype(BF16)
    tp_send(own_up, uall, 2)
    tp_send(e_block, erecv, 6)

    tp_wait(own_lin, linall, 4, True)
    values = fdot(back, linall[...].reshape(n_tp * slot_pad, width))
    centered = values - jnp.mean(values, axis=1, keepdims=True)
    variance = jnp.mean(centered * centered, axis=1, keepdims=True)
    normed = centered / jnp.sqrt(variance + 1e-05) * gain[...] + bias[...]
    normed_t = jnp.transpose(normed)
    for d in range(n_dp):
        nts[d] = normed_t[d * depth : (d + 1) * depth].astype(BF16)
    normed = normed.astype(BF16)
    for i in range(1, n_dp):
        to = (me_dp + i) % n_dp
        remote(nts.at[to], ntr.at[me_dp], dsem.at[0, to], dsem.at[1, me_dp], {"dp": to}).start()
    ntr[me_dp] = nts[me_dp]

    loads[2].wait()

    def forward(i, carry):
        columns = pl.ds(pl.multiple_of(i * step_h, step_h), step_h) if step_h != hid else slice(None)
        preact = fdot(normed, w1[:, columns]) + b1[:, columns]
        cdf = 0.5 * (1.0 + lax.erf(preact * 0.7071067811865476))
        density = jnp.exp(-0.5 * preact * preact) * 0.3989422804014327
        hidden[:, columns] = (preact * cdf).astype(BF16)
        deriv[:, columns] = cdf + preact * density
        return carry

    lax.fori_loop(0, hid // step_h, forward, 0)

    loads[3].wait()
    tp_wait(own_up, uall, 2, True)
    gather = onehot(rows, n_tp * share_pad, pad_col, 1)
    up_f = fdot(gather, uall[...].reshape(n_tp * share_pad, width))
    up = up_f.astype(BF16)

    def backward(i, carry):
        columns = pl.ds(pl.multiple_of(i * step_h, step_h), step_h) if step_h != hid else slice(None)
        grads[me_dp, :, columns] = (fdot(up, w2[:, columns]) * deriv[:, columns]).astype(BF16)
        return carry

    lax.fori_loop(0, hid // step_h, backward, 0)

    spots = (z, nz - 1 - z)
    ahead = ({"dp": (z + 1) * CORES + core}, {"dp": (z - 1) * CORES + core})

    def real(way, at):
        return at if way == 0 else nz - 1 - at

    def block_copy(way, chip):
        block = grads.at[chip * CORES + core]
        return remote(block, block, zsem.at[way, chip], zsem.at[2 + way, chip], ahead[way])

    def chain_copy(way, owner):
        block = chain.at[way, owner]
        return remote(block, block, zsem.at[4 + way, owner], zsem.at[6 + way, owner], ahead[way])

    def partner_copy(chip, side):
        block = grads.at[chip * CORES + side]
        return remote(block, block, zsem.at[8, chip], zsem.at[9, chip], partner)

    def cross_copy(chip):
        return remote(
            terms.at[chip * CORES + 1 - core], cross.at[chip], zsem.at[10, chip], zsem.at[11, chip], partner
        )

    def send_block(step):
        for way in (0, 1):
            @pl.when((spots[way] >= step) & (spots[way] < nz - 1))
            def _():
                block_copy(way, real(way, spots[way] - step)).start()

    send_block(0)
    partner_copy(z, core).start()

    up_t = jnp.transpose(up_f)
    for d in range(n_dp):
        upt[d] = up_t[d * depth : (d + 1) * depth].astype(BF16)

    def term(d):
        terms[d] = (fdot(upt[d], hidden[...]) * factor).astype(BF16)

    def other_terms(chip, carry):
        term(chip * CORES + 1 - core)
        cross_copy(chip).start()
        return carry

    def own_terms(chip, carry):
        term(chip * CORES + core)
        return carry

    lax.fori_loop(0, nz, other_terms, 0)
    lax.fori_loop(0, nz, own_terms, 0)

    def merge(chip, carry):
        cross_copy(chip).wait_recv()
        own = terms[chip * CORES + core].astype(F32)
        cross[chip] = (own + cross[chip].astype(F32)).astype(BF16)
        return carry

    lax.fori_loop(0, nz, merge, 0)

    for step in range(nz - 1):
        if step:
            send_block(step)
        for way in (0, 1):
            spot = spots[way]
            owner = real(way, nz - 1 + spot - step)

            @pl.when((spot <= step) & (spot == 0))
            def _():
                chain[way, owner] = cross[owner]
                chain_copy(way, owner).start()

            @pl.when((spot <= step) & (spot > 0))
            def _():
                chain_copy(way, owner).wait_recv()
                chain[way, owner] = (chain[way, owner].astype(F32) + cross[owner].astype(F32)).astype(BF16)
                chain_copy(way, owner).start()

        for way in (0, 1):
            @pl.when(spots[way] > step)
            def _():
                chip = real(way, spots[way] - 1 - step)
                block_copy(way, chip).wait_recv()
                partner_copy(chip, core).start()

    tp_wait(e_block, erecv, 6, True)

    def collect(i, carry):
        columns = pl.ds(pl.multiple_of(i * width, 128), width)
        early = esend[me_tp, :, columns].astype(F32)
        for j in range(1, n_tp):
            early = early + erecv[(me_tp + j) % n_tp, :, columns].astype(F32)
        early_o[:, columns] = early.astype(BF16)
        return carry

    lax.fori_loop(0, parte.shape[1] // width, collect, 0)

    for i in range(1, n_dp):
        to = (me_dp + i) % n_dp
        remote(nts.at[to], ntr.at[to], dsem.at[0, to], dsem.at[1, to], {"dp": to}).wait_recv()

    for chip in range(nz):
        partner_copy(chip, 1 - core).wait_recv()
    first = fdot(ntr[0], grads[0])
    for k in range(1, n_dp):
        first = first + fdot(ntr[k], grads[k])
    g1_o[...] = (first * factor).astype(BF16)

    for way in (0, 1):
        @pl.when(spots[way] > 0)
        def _():
            chain_copy(way, z).wait_recv()

        @pl.when(spots[way] == 0)
        def _():
            chain[way, z] = jnp.zeros_like(chain[way, z])

    second = cross[z].astype(F32) + chain[0, z].astype(F32) + chain[1, z].astype(F32)
    g2_o[...] = second.astype(BF16)

    tp_wait(u_block, urecv, 0, False)
    tp_wait(own_up, uall, 2, False)
    tp_wait(own_lin, linall, 4, False)
    tp_wait(e_block, erecv, 6, False)
    for i in range(1, n_dp):
        to = (me_dp + i) % n_dp
        remote(nts.at[to], ntr.at[to], dsem.at[0, to], dsem.at[1, to], {"dp": to}).wait_send()
    for chip in range(nz):
        partner_copy(chip, core).wait_send()
        cross_copy(chip).wait_send()
    for step in range(nz - 1):
        for way in (0, 1):
            spot = spots[way]

            @pl.when((spot >= step) & (spot < nz - 1))
            def _():
                block_copy(way, real(way, spot - step)).wait_send()

            @pl.when(spot <= step)
            def _():
                chain_copy(way, real(way, nz - 1 + spot - step)).wait_send()


def shards(partials, layer_input, ln_gain, ln_bias, fc1_weight, fc1_bias, fc2_weight, row_rank):
    n_tp = lax.axis_size("tp")
    n_dp = lax.axis_size("dp")
    nz = n_dp // CORES
    part = partials[0]
    rows, vis = part.shape
    slots, width = layer_input.shape
    hid = fc1_weight.shape[1]
    slot_pad = up_to(slots, 16)
    share = -(-rows // n_tp)
    share_pad = up_to(share, 16)
    depth = width // n_dp
    rest = vis - width
    vmem = pl.BlockSpec(memory_space=pltpu.VMEM)
    anywhere = pl.BlockSpec(memory_space=pl.ANY)
    padded = jnp.pad(layer_input, ((0, slot_pad - slots), (0, 0)))
    early, first, second = pl.pallas_call(
        functools.partial(kernel, n_tp, n_dp, share, float(n_dp * rows) ** (-0.5)),
        out_shape=(
            jax.ShapeDtypeStruct((slot_pad, rest), BF16),
            jax.ShapeDtypeStruct((depth, hid), BF16),
            jax.ShapeDtypeStruct((depth, hid), BF16),
        ),
        in_specs=[vmem, vmem, anywhere, vmem, vmem, vmem, anywhere, vmem, anywhere],
        out_specs=(vmem, vmem, vmem),
        scratch_shapes=[
            pltpu.VMEM((rows, width), BF16),
            pltpu.VMEM((rows, rest), BF16),
            pltpu.VMEM((width, hid), BF16),
            pltpu.VMEM((width, hid), BF16),
            pltpu.VMEM((n_tp, slot_pad, width), BF16),
            pltpu.VMEM((n_tp, share_pad, width), BF16),
            pltpu.VMEM((n_tp, share_pad, width), BF16),
            pltpu.VMEM((n_tp, share_pad, width), BF16),
            pltpu.VMEM((n_tp, slot_pad, rest), BF16),
            pltpu.VMEM((n_tp, slot_pad, rest), BF16),
            pltpu.VMEM((rows, hid), BF16),
            pltpu.VMEM((rows, hid), F32),
            pltpu.VMEM((n_dp, depth, rows), BF16),
            pltpu.VMEM((n_dp, depth, rows), BF16),
            pltpu.VMEM((n_dp, depth, rows), BF16),
            pltpu.VMEM((n_dp, depth, hid), BF16),
            pltpu.VMEM((nz, depth, hid), BF16),
            pltpu.VMEM((2, nz, depth, hid), BF16),
            pltpu.VMEM((n_dp, rows, hid), BF16),
            pltpu.SemaphoreType.DMA((4,)),
            pltpu.SemaphoreType.DMA((8, n_tp)),
            pltpu.SemaphoreType.DMA((2, n_dp)),
            pltpu.SemaphoreType.DMA((12, nz)),
        ],
        compiler_params=pltpu.CompilerParams(
            collective_id=0, has_side_effects=True, vmem_limit_bytes=58 * 1024 * 1024
        ),
        name="route_and_grads",
    )(
        row_rank.reshape(1, rows),
        row_rank,
        part,
        padded,
        ln_gain.reshape(1, width),
        ln_bias.reshape(1, width),
        fc1_weight,
        fc1_bias.reshape(1, hid),
        fc2_weight,
    )
    return early[:slots], first, second


def solution(mesh):
    return jax.shard_map(
        shards,
        mesh=mesh,
        in_specs=(
            P("tp", "dp", None),
            P(("dp", "tp"), None),
            P(),
            P(),
            P(None, "tp"),
            P("tp"),
            P(None, "tp"),
            P("dp", None),
        ),
        out_specs=(P(("dp", "tp"), None), P("dp", "tp"), P("dp", "tp")),
        check_vma=False,
    )
```

```python
import functools

import jax
import jax.numpy as jnp
from jax import lax
from jax.experimental import pallas as pl
from jax.experimental.pallas import tpu as pltpu
from jax.sharding import PartitionSpec as P

MESH = pl.DeviceIdType.MESH
CORES = 2
F32 = jnp.float32
BF16 = jnp.bfloat16


def up_to(value, step):
    return -(-value // step) * step


def onehot(rows, columns, wanted, axis):
    at = lax.broadcasted_iota(jnp.int32, (rows, columns), axis).astype(F32)
    return jnp.where(at == wanted, 1.0, 0.0).astype(BF16)


def fdot(left, right):
    return jnp.dot(left, right, preferred_element_type=F32)


def kernel(
    n_tp, n_dp, share, factor,
    rank_row, part, lin_own, gain, bias, fc1, b1, fc2,
    early_o, g1_o, g2_o,
    partu, parte, w1, w2, lin_wide, lin, linall, usend, urecv, uall, esend, erecv,
    hidden, deriv, nts, ntr, upt, terms, cross, chain, grads,
    lsem, tsem, dsem, zsem,
):
    me_tp = lax.axis_index("tp")
    me_dp = lax.axis_index("dp")
    z, core = me_dp // CORES, me_dp % CORES
    nz = n_dp // CORES
    partner = {"dp": z * CORES + 1 - core}
    rows, width = partu.shape
    slot_pad = lin.shape[0]
    share_pad = usend.shape[1]
    hid = w1.shape[1]
    depth = g1_o.shape[0]
    step_h = 256 if hid % 256 == 0 else hid

    loads = [
        pltpu.make_async_copy(part.at[:, pl.ds(0, width)], partu, lsem.at[0]),
        pltpu.make_async_copy(part.at[:, pl.ds(width, parte.shape[1])], parte, lsem.at[1]),
        pltpu.make_async_copy(fc1, w1, lsem.at[2]),
        pltpu.make_async_copy(fc2, w2, lsem.at[3]),
    ]
    for load in loads:
        load.start()

    barrier = pltpu.get_barrier_semaphore()
    for i in range(1, n_tp):
        pl.semaphore_signal(barrier, inc=1, device_id={"tp": (me_tp + i) % n_tp}, device_id_type=MESH)
    for i in range(1, n_dp):
        pl.semaphore_signal(barrier, inc=1, device_id={"dp": (me_dp + i) % n_dp}, device_id_type=MESH)
    pl.semaphore_wait(barrier, n_tp + n_dp - 2)

    def remote(src, dst, send, recv, device):
        return pltpu.make_async_remote_copy(
            src_ref=src, dst_ref=dst, send_sem=send, recv_sem=recv, device_id=device, device_id_type=MESH
        )

    def tp_send(src_of, dst, kind):
        for i in range(1, n_tp):
            to = (me_tp + i) % n_tp
            remote(src_of(to), dst.at[me_tp], tsem.at[kind, to], tsem.at[kind + 1, me_tp], {"tp": to}).start()

    def tp_wait(src_of, dst, kind, recv):
        for i in range(1, n_tp):
            to = (me_tp + i) % n_tp
            copy = remote(src_of(to), dst.at[to], tsem.at[kind, to], tsem.at[kind + 1, to], {"tp": to})
            if recv:
                copy.wait_recv()
            else:
                copy.wait_send()

    slots = lin_own.shape[0]
    lin_wide[0:slots, :] = lin_own[...].astype(F32)
    if slot_pad > slots:
        lin_wide[slots:slot_pad, :] = jnp.zeros((slot_pad - slots, width), F32)
    lin[...] = lin_wide[...].astype(BF16)

    own_lin = lambda to: lin
    u_block = lambda to: usend.at[to]
    own_up = lambda to: uall.at[me_tp]
    e_block = lambda to: esend.at[to]

    r_row = lax.broadcasted_iota(jnp.int32, (1, rows), 1)
    r_col = lax.broadcasted_iota(jnp.int32, (rows, 1), 0)
    pad_row, pad_col = (r_row * 0).astype(F32), (r_col * 0).astype(F32)
    for i in range(1, n_tp):
        pad_row = pad_row + jnp.where(r_row >= i * share, 1.0, 0.0)
        pad_col = pad_col + jnp.where(r_col >= i * share, 1.0, 0.0)
    pad_row = r_row.astype(F32) + pad_row * (share_pad - share)
    pad_col = r_col.astype(F32) + pad_col * (share_pad - share)

    loads[0].wait()
    spread = onehot(n_tp * share_pad, rows, pad_row, 0)
    usend[...] = fdot(spread, partu[...]).astype(BF16).reshape(usend.shape)
    tp_send(u_block, urecv, 0)
    tp_send(own_lin, linall, 4)
    linall[me_tp] = lin[...]

    at0 = lax.broadcasted_iota(jnp.int32, (rows, rows), 0)
    at1 = lax.broadcasted_iota(jnp.int32, (rows, rows), 1)
    rank_r = rank_row[...].astype(F32)
    rank_c = jnp.sum(jnp.where(at0 == at1, rank_r, 0.0), axis=1, keepdims=True)
    same = rank_c == rank_r
    place_r = jnp.sum(jnp.where(same & (at0 < at1), 1.0, 0.0), axis=0, keepdims=True)
    place_c = jnp.sum(jnp.where(same & (at1 < at0), 1.0, 0.0), axis=1, keepdims=True)
    slot_r = rank_r * slot_pad + place_r
    slot_c = rank_c * slot_pad + place_c
    table = onehot(n_tp * slot_pad, rows, slot_r, 0)
    back = onehot(rows, n_tp * slot_pad, slot_c, 1)

    loads[1].wait()

    def place(i, carry):
        columns = pl.ds(pl.multiple_of(i * width, 128), width)
        placed = fdot(table, parte[:, columns]).astype(BF16)
        esend[:, :, columns] = placed.reshape(n_tp, slot_pad, width)
        return carry

    lax.fori_loop(0, parte.shape[1] // width, place, 0)

    tp_wait(u_block, urecv, 0, True)
    total = usend[me_tp].astype(F32)
    for i in range(1, n_tp):
        total = total + urecv[(me_tp + i) % n_tp].astype(F32)
    uall[me_tp] = total.astype(BF16)
    tp_send(own_up, uall, 2)
    tp_send(e_block, erecv, 6)

    tp_wait(own_lin, linall, 4, True)
    values = fdot(back, linall[...].reshape(n_tp * slot_pad, width))
    centered = values - jnp.mean(values, axis=1, keepdims=True)
    variance = jnp.mean(centered * centered, axis=1, keepdims=True)
    normed = centered / jnp.sqrt(variance + 1e-05) * gain[...].reshape(1, width) + bias[...].reshape(1, width)
    normed_t = jnp.transpose(normed)
    for d in range(n_dp):
        nts[d] = normed_t[d * depth : (d + 1) * depth].astype(BF16)
    normed = normed.astype(BF16)
    for i in range(1, n_dp):
        to = (me_dp + i) % n_dp
        remote(nts.at[to], ntr.at[me_dp], dsem.at[0, to], dsem.at[1, me_dp], {"dp": to}).start()
    ntr[me_dp] = nts[me_dp]

    loads[2].wait()

    def forward(i, carry):
        columns = pl.ds(pl.multiple_of(i * step_h, step_h), step_h) if step_h != hid else slice(None)
        preact = fdot(normed, w1[:, columns]) + b1[columns].reshape(1, step_h)
        cdf = 0.5 * (1.0 + lax.erf(preact * 0.7071067811865476))
        density = jnp.exp(-0.5 * preact * preact) * 0.3989422804014327
        hidden[:, columns] = (preact * cdf).astype(BF16)
        deriv[:, columns] = cdf + preact * density
        return carry

    lax.fori_loop(0, hid // step_h, forward, 0)

    loads[3].wait()
    tp_wait(own_up, uall, 2, True)
    gather = onehot(rows, n_tp * share_pad, pad_col, 1)
    up_f = fdot(gather, uall[...].reshape(n_tp * share_pad, width))
    up = up_f.astype(BF16)

    def backward(i, carry):
        columns = pl.ds(pl.multiple_of(i * step_h, step_h), step_h) if step_h != hid else slice(None)
        grads[me_dp, :, columns] = (fdot(up, w2[:, columns]) * deriv[:, columns]).astype(BF16)
        return carry

    lax.fori_loop(0, hid // step_h, backward, 0)

    spots = (z, nz - 1 - z)
    ahead = ({"dp": (z + 1) * CORES + core}, {"dp": (z - 1) * CORES + core})

    def real(way, at):
        return at if way == 0 else nz - 1 - at

    def block_copy(way, chip):
        block = grads.at[chip * CORES + core]
        return remote(block, block, zsem.at[way, chip], zsem.at[2 + way, chip], ahead[way])

    def chain_copy(way, owner):
        block = chain.at[way, owner]
        return remote(block, block, zsem.at[4 + way, owner], zsem.at[6 + way, owner], ahead[way])

    def partner_copy(chip, side):
        block = grads.at[chip * CORES + side]
        return remote(block, block, zsem.at[8, chip], zsem.at[9, chip], partner)

    def cross_copy(chip):
        return remote(
            terms.at[chip * CORES + 1 - core], cross.at[chip], zsem.at[10, chip], zsem.at[11, chip], partner
        )

    def send_block(step):
        for way in (0, 1):
            @pl.when((spots[way] >= step) & (spots[way] < nz - 1))
            def _():
                block_copy(way, real(way, spots[way] - step)).start()

    send_block(0)
    partner_copy(z, core).start()

    up_t = jnp.transpose(up_f)
    for d in range(n_dp):
        upt[d] = up_t[d * depth : (d + 1) * depth].astype(BF16)

    def term(d):
        terms[d] = (fdot(upt[d], hidden[...]) * factor).astype(BF16)

    def other_terms(chip, carry):
        term(chip * CORES + 1 - core)
        cross_copy(chip).start()
        return carry

    def own_terms(chip, carry):
        term(chip * CORES + core)
        return carry

    lax.fori_loop(0, nz, other_terms, 0)
    lax.fori_loop(0, nz, own_terms, 0)

    def merge(chip, carry):
        cross_copy(chip).wait_recv()
        own = terms[chip * CORES + core].astype(F32)
        cross[chip] = (own + cross[chip].astype(F32)).astype(BF16)
        return carry

    lax.fori_loop(0, nz, merge, 0)

    for step in range(nz - 1):
        if step:
            send_block(step)
        for way in (0, 1):
            spot = spots[way]
            owner = real(way, nz - 1 + spot - step)

            @pl.when((spot <= step) & (spot == 0))
            def _():
                chain[way, owner] = cross[owner]
                chain_copy(way, owner).start()

            @pl.when((spot <= step) & (spot > 0))
            def _():
                chain_copy(way, owner).wait_recv()
                chain[way, owner] = (chain[way, owner].astype(F32) + cross[owner].astype(F32)).astype(BF16)
                chain_copy(way, owner).start()

        for way in (0, 1):
            @pl.when(spots[way] > step)
            def _():
                chip = real(way, spots[way] - 1 - step)
                block_copy(way, chip).wait_recv()
                partner_copy(chip, core).start()

    tp_wait(e_block, erecv, 6, True)

    def collect(i, carry):
        columns = pl.ds(pl.multiple_of(i * width, 128), width)
        early = esend[me_tp, :, columns].astype(F32)
        for j in range(1, n_tp):
            early = early + erecv[(me_tp + j) % n_tp, :, columns].astype(F32)
        early_o[:, columns] = early.astype(BF16)
        return carry

    lax.fori_loop(0, parte.shape[1] // width, collect, 0)

    for i in range(1, n_dp):
        to = (me_dp + i) % n_dp
        remote(nts.at[to], ntr.at[to], dsem.at[0, to], dsem.at[1, to], {"dp": to}).wait_recv()

    for chip in range(nz):
        partner_copy(chip, 1 - core).wait_recv()
    first = fdot(ntr[0], grads[0])
    for k in range(1, n_dp):
        first = first + fdot(ntr[k], grads[k])
    g1_o[...] = (first * factor).astype(BF16)

    for way in (0, 1):
        @pl.when(spots[way] > 0)
        def _():
            chain_copy(way, z).wait_recv()

        @pl.when(spots[way] == 0)
        def _():
            chain[way, z] = jnp.zeros_like(chain[way, z])

    second = cross[z].astype(F32) + chain[0, z].astype(F32) + chain[1, z].astype(F32)
    g2_o[...] = second.astype(BF16)

    tp_wait(u_block, urecv, 0, False)
    tp_wait(own_up, uall, 2, False)
    tp_wait(own_lin, linall, 4, False)
    tp_wait(e_block, erecv, 6, False)
    for i in range(1, n_dp):
        to = (me_dp + i) % n_dp
        remote(nts.at[to], ntr.at[to], dsem.at[0, to], dsem.at[1, to], {"dp": to}).wait_send()
    for chip in range(nz):
        partner_copy(chip, core).wait_send()
        cross_copy(chip).wait_send()
    for step in range(nz - 1):
        for way in (0, 1):
            spot = spots[way]

            @pl.when((spot >= step) & (spot < nz - 1))
            def _():
                block_copy(way, real(way, spot - step)).wait_send()

            @pl.when(spot <= step)
            def _():
                chain_copy(way, real(way, nz - 1 + spot - step)).wait_send()


def finish(early, first, second, early_o, first_o, second_o):
    early_o[...] = early[0 : early_o.shape[0], :]
    first_o[...] = first[...]
    second_o[...] = second[...]


def shards(partials, layer_input, ln_gain, ln_bias, fc1_weight, fc1_bias, fc2_weight, row_rank):
    n_tp = lax.axis_size("tp")
    n_dp = lax.axis_size("dp")
    nz = n_dp // CORES
    part = partials[0]
    rows, vis = part.shape
    slots, width = layer_input.shape
    hid = fc1_weight.shape[1]
    slot_pad = up_to(slots, 16)
    share = -(-rows // n_tp)
    share_pad = up_to(share, 16)
    depth = width // n_dp
    rest = vis - width
    vmem = pl.BlockSpec(memory_space=pltpu.VMEM)
    anywhere = pl.BlockSpec(memory_space=pl.ANY)
    early, first, second = pl.pallas_call(
        functools.partial(kernel, n_tp, n_dp, share, float(n_dp * rows) ** (-0.5)),
        out_shape=(
            jax.ShapeDtypeStruct((slot_pad, rest), BF16),
            jax.ShapeDtypeStruct((depth, hid), BF16),
            jax.ShapeDtypeStruct((depth, hid), BF16),
        ),
        in_specs=[vmem, anywhere, vmem, vmem, vmem, anywhere, vmem, anywhere],
        out_specs=(vmem, vmem, vmem),
        scratch_shapes=[
            pltpu.VMEM((rows, width), BF16),
            pltpu.VMEM((rows, rest), BF16),
            pltpu.VMEM((width, hid), BF16),
            pltpu.VMEM((width, hid), BF16),
            pltpu.VMEM((slot_pad, width), F32),
            pltpu.VMEM((slot_pad, width), BF16),
            pltpu.VMEM((n_tp, slot_pad, width), BF16),
            pltpu.VMEM((n_tp, share_pad, width), BF16),
            pltpu.VMEM((n_tp, share_pad, width), BF16),
            pltpu.VMEM((n_tp, share_pad, width), BF16),
            pltpu.VMEM((n_tp, slot_pad, rest), BF16),
            pltpu.VMEM((n_tp, slot_pad, rest), BF16),
            pltpu.VMEM((rows, hid), BF16),
            pltpu.VMEM((rows, hid), F32),
            pltpu.VMEM((n_dp, depth, rows), BF16),
            pltpu.VMEM((n_dp, depth, rows), BF16),
            pltpu.VMEM((n_dp, depth, rows), BF16),
            pltpu.VMEM((n_dp, depth, hid), BF16),
            pltpu.VMEM((nz, depth, hid), BF16),
            pltpu.VMEM((2, nz, depth, hid), BF16),
            pltpu.VMEM((n_dp, rows, hid), BF16),
            pltpu.SemaphoreType.DMA((4,)),
            pltpu.SemaphoreType.DMA((8, n_tp)),
            pltpu.SemaphoreType.DMA((2, n_dp)),
            pltpu.SemaphoreType.DMA((12, nz)),
        ],
        compiler_params=pltpu.CompilerParams(
            collective_id=0, has_side_effects=True, vmem_limit_bytes=58 * 1024 * 1024
        ),
        name="route_and_grads",
    )(
        row_rank.reshape(1, rows),
        part,
        layer_input,
        ln_gain,
        ln_bias,
        fc1_weight,
        fc1_bias,
        fc2_weight,
    )
    return pl.pallas_call(
        finish,
        out_shape=(
            jax.ShapeDtypeStruct((slots, rest), BF16),
            jax.ShapeDtypeStruct((depth, hid), BF16),
            jax.ShapeDtypeStruct((depth, hid), BF16),
        ),
        in_specs=[vmem, vmem, vmem],
        out_specs=(vmem, vmem, vmem),
        name="finish",
    )(early, first, second)


def solution(mesh):
    return jax.shard_map(
        shards,
        mesh=mesh,
        in_specs=(
            P("tp", "dp", None),
            P(("dp", "tp"), None),
            P(),
            P(),
            P(None, "tp"),
            P("tp"),
            P(None, "tp"),
            P("dp", None),
        ),
        out_specs=(P(("dp", "tp"), None), P("dp", "tp"), P("dp", "tp")),
        check_vma=False,
    )
```

```python
import functools

import jax
import jax.numpy as jnp
from jax import lax
from jax.experimental import pallas as pl
from jax.experimental.pallas import tpu as pltpu
from jax.sharding import PartitionSpec as P

MESH = pl.DeviceIdType.MESH
CORES = 2
F32 = jnp.float32
BF16 = jnp.bfloat16


def up_to(value, step):
    return -(-value // step) * step


def onehot(rows, columns, wanted, axis):
    at = lax.broadcasted_iota(jnp.int32, (rows, columns), axis).astype(F32)
    return jnp.where(at == wanted, 1.0, 0.0).astype(BF16)


def fdot(left, right):
    return jnp.dot(left, right, preferred_element_type=F32)


def kernel(
    n_tp, n_dp, outer, share, factor,
    rank_row, part, lin_own, gain, bias, fc1, b1, fc2,
    early_o, g1_o, g2_o,
    partu, parte, w1, w2, lin_wide, lin, linall, usend, urecv, uall, esend, near, far,
    hidden, deriv, nts, ntr, upt, terms, cross, chain, grads,
    lsem, tsem, esem, dsem, zsem,
):
    me_tp = lax.axis_index("tp")
    me_dp = lax.axis_index("dp")
    z, core = me_dp // CORES, me_dp % CORES
    nz = n_dp // CORES
    partner = {"dp": z * CORES + 1 - core}
    rows, width = partu.shape
    slot_pad = lin.shape[0]
    share_pad = usend.shape[1]
    hid = w1.shape[1]
    depth = g1_o.shape[0]
    step_h = 256 if hid % 256 == 0 else hid

    loads = [
        pltpu.make_async_copy(part.at[:, pl.ds(0, width)], partu, lsem.at[0]),
        pltpu.make_async_copy(part.at[:, pl.ds(width, parte.shape[1])], parte, lsem.at[1]),
        pltpu.make_async_copy(fc1, w1, lsem.at[2]),
        pltpu.make_async_copy(fc2, w2, lsem.at[3]),
    ]
    for load in loads:
        load.start()

    barrier = pltpu.get_barrier_semaphore()
    for i in range(1, n_tp):
        pl.semaphore_signal(barrier, inc=1, device_id={"tp": (me_tp + i) % n_tp}, device_id_type=MESH)
    for i in range(1, n_dp):
        pl.semaphore_signal(barrier, inc=1, device_id={"dp": (me_dp + i) % n_dp}, device_id_type=MESH)
    pl.semaphore_wait(barrier, n_tp + n_dp - 2)

    def remote(src, dst, send, recv, device):
        return pltpu.make_async_remote_copy(
            src_ref=src, dst_ref=dst, send_sem=send, recv_sem=recv, device_id=device, device_id_type=MESH
        )

    def tp_send(src_of, dst, kind):
        for i in range(1, n_tp):
            to = (me_tp + i) % n_tp
            remote(src_of(to), dst.at[me_tp], tsem.at[kind, to], tsem.at[kind + 1, me_tp], {"tp": to}).start()

    def tp_wait(src_of, dst, kind, recv):
        for i in range(1, n_tp):
            to = (me_tp + i) % n_tp
            copy = remote(src_of(to), dst.at[to], tsem.at[kind, to], tsem.at[kind + 1, to], {"tp": to})
            if recv:
                copy.wait_recv()
            else:
                copy.wait_send()

    slots = lin_own.shape[0]
    lin_wide[0:slots, :] = lin_own[...].astype(F32)
    if slot_pad > slots:
        lin_wide[slots:slot_pad, :] = jnp.zeros((slot_pad - slots, width), F32)
    lin[...] = lin_wide[...].astype(BF16)

    own_lin = lambda to: lin
    u_block = lambda to: usend.at[to]
    own_up = lambda to: uall.at[me_tp]

    inner = n_tp // outer
    place_a, place_b = me_tp // inner, me_tp % inner
    half = esend.shape[2] // 2

    def axes(way):
        return ((place_b, inner), (place_a, outer)) if way == 0 else ((place_a, outer), (place_b, inner))

    def rank_of(way, first, second):
        return second * inner + first if way == 0 else first * inner + second

    def e_half(way, rank):
        return esend.at[rank, :, pl.ds(way * half, half)]

    def near_copy(way, i, other, sending):
        (first, extent), (second, count) = axes(way)
        peer = (first + i) % extent
        held = first if sending else peer
        return remote(
            e_half(way, rank_of(way, peer, other)),
            near.at[way, held * count + other],
            esem.at[way, peer * count + other],
            esem.at[2 + way, held * count + other],
            {"tp": rank_of(way, peer, second)},
        )

    def far_copy(way, i, sending):
        (first, extent), (second, count) = axes(way)
        peer = (second + i) % count
        held = second if sending else peer
        return remote(
            e_half(way, rank_of(way, first, peer)),
            far.at[way, held],
            esem.at[4 + way, peer],
            esem.at[6 + way, held],
            {"tp": rank_of(way, first, peer)},
        )

    def near_all(act):
        for other in range(n_tp):
            for way in (0, 1):
                (_, extent), (_, count) = axes(way)
                if other < count:
                    for i in range(1, extent):
                        act(near_copy(way, i, other, False))

    def near_start():
        for other in range(n_tp):
            for way in (0, 1):
                (_, extent), (_, count) = axes(way)
                if other < count:
                    for i in range(1, extent):
                        near_copy(way, i, other, True).start()

    def near_sum():
        near_all(lambda copy: copy.wait_recv())
        for way in (0, 1):
            (first, extent), (second, count) = axes(way)
            for i in list(range(1, count)) + [0]:
                other = (second + i) % count
                spot = rank_of(way, first, other)

                def add(c, carry):
                    columns = pl.ds(pl.multiple_of(c * chunk, 128), chunk)
                    mine = pl.ds(pl.multiple_of(way * half + c * chunk, 128), chunk)
                    block = esend[spot, :, mine].astype(F32)
                    for j in range(1, extent):
                        block = block + near[way, ((first + j) % extent) * count + other, :, columns].astype(F32)
                    esend[spot, :, mine] = block.astype(BF16)
                    return carry

                lax.fori_loop(0, half // chunk, add, 0)
                if i:
                    far_copy(way, i, True).start()

    def far_sum():
        for way in (0, 1):
            (first, extent), (second, count) = axes(way)
            for i in range(1, count):
                far_copy(way, i, False).wait_recv()

            def add(c, carry):
                columns = pl.ds(pl.multiple_of(c * chunk, 128), chunk)
                mine = pl.ds(pl.multiple_of(way * half + c * chunk, 128), chunk)
                block = esend[me_tp, :, mine].astype(F32)
                for j in range(1, count):
                    block = block + far[way, (second + j) % count, :, columns].astype(F32)
                early_o[:, mine] = block.astype(BF16)
                return carry

            lax.fori_loop(0, half // chunk, add, 0)

    def early_sent():
        near_all(lambda copy: copy.wait_send())
        for way in (0, 1):
            _, (_, count) = axes(way)
            for i in range(1, count):
                far_copy(way, i, False).wait_send()

    chunk = 640 if half % 640 == 0 else half

    r_row = lax.broadcasted_iota(jnp.int32, (1, rows), 1)
    r_col = lax.broadcasted_iota(jnp.int32, (rows, 1), 0)
    pad_row, pad_col = (r_row * 0).astype(F32), (r_col * 0).astype(F32)
    for i in range(1, n_tp):
        pad_row = pad_row + jnp.where(r_row >= i * share, 1.0, 0.0)
        pad_col = pad_col + jnp.where(r_col >= i * share, 1.0, 0.0)
    pad_row = r_row.astype(F32) + pad_row * (share_pad - share)
    pad_col = r_col.astype(F32) + pad_col * (share_pad - share)

    loads[0].wait()
    spread = onehot(n_tp * share_pad, rows, pad_row, 0)
    usend[...] = fdot(spread, partu[...]).astype(BF16).reshape(usend.shape)
    tp_send(u_block, urecv, 0)
    tp_send(own_lin, linall, 4)
    linall[me_tp] = lin[...]

    at0 = lax.broadcasted_iota(jnp.int32, (rows, rows), 0)
    at1 = lax.broadcasted_iota(jnp.int32, (rows, rows), 1)
    rank_r = rank_row[...].astype(F32)
    rank_c = jnp.sum(jnp.where(at0 == at1, rank_r, 0.0), axis=1, keepdims=True)
    same = rank_c == rank_r
    place_r = jnp.sum(jnp.where(same & (at0 < at1), 1.0, 0.0), axis=0, keepdims=True)
    place_c = jnp.sum(jnp.where(same & (at1 < at0), 1.0, 0.0), axis=1, keepdims=True)
    slot_r = rank_r * slot_pad + place_r
    slot_c = rank_c * slot_pad + place_c
    table = onehot(n_tp * slot_pad, rows, slot_r, 0)
    back = onehot(rows, n_tp * slot_pad, slot_c, 1)

    loads[1].wait()

    def place(i, carry):
        columns = pl.ds(pl.multiple_of(i * width, 128), width)
        placed = fdot(table, parte[:, columns]).astype(BF16)
        esend[:, :, columns] = placed.reshape(n_tp, slot_pad, width)
        return carry

    lax.fori_loop(0, parte.shape[1] // width, place, 0)

    tp_wait(u_block, urecv, 0, True)
    total = usend[me_tp].astype(F32)
    for i in range(1, n_tp):
        total = total + urecv[(me_tp + i) % n_tp].astype(F32)
    uall[me_tp] = total.astype(BF16)
    tp_send(own_up, uall, 2)
    near_start()

    tp_wait(own_lin, linall, 4, True)
    values = fdot(back, linall[...].reshape(n_tp * slot_pad, width))
    centered = values - jnp.mean(values, axis=1, keepdims=True)
    variance = jnp.mean(centered * centered, axis=1, keepdims=True)
    normed = centered / jnp.sqrt(variance + 1e-05) * gain[...].reshape(1, width) + bias[...].reshape(1, width)
    normed_t = jnp.transpose(normed)
    for d in range(n_dp):
        nts[d] = normed_t[d * depth : (d + 1) * depth].astype(BF16)
    normed = normed.astype(BF16)
    for i in range(1, n_dp):
        to = (me_dp + i) % n_dp
        remote(nts.at[to], ntr.at[me_dp], dsem.at[0, to], dsem.at[1, me_dp], {"dp": to}).start()
    ntr[me_dp] = nts[me_dp]

    loads[2].wait()

    def forward(i, carry):
        columns = pl.ds(pl.multiple_of(i * step_h, step_h), step_h) if step_h != hid else slice(None)
        preact = fdot(normed, w1[:, columns]) + b1[columns].reshape(1, step_h)
        cdf = 0.5 * (1.0 + lax.erf(preact * 0.7071067811865476))
        density = jnp.exp(-0.5 * preact * preact) * 0.3989422804014327
        hidden[:, columns] = (preact * cdf).astype(BF16)
        deriv[:, columns] = cdf + preact * density
        return carry

    lax.fori_loop(0, hid // step_h, forward, 0)

    loads[3].wait()
    tp_wait(own_up, uall, 2, True)
    gather = onehot(rows, n_tp * share_pad, pad_col, 1)
    up_f = fdot(gather, uall[...].reshape(n_tp * share_pad, width))
    up = up_f.astype(BF16)

    def backward(i, carry):
        columns = pl.ds(pl.multiple_of(i * step_h, step_h), step_h) if step_h != hid else slice(None)
        grads[me_dp, :, columns] = (fdot(up, w2[:, columns]) * deriv[:, columns]).astype(BF16)
        return carry

    lax.fori_loop(0, hid // step_h, backward, 0)

    spots = (z, nz - 1 - z)
    ahead = ({"dp": (z + 1) * CORES + core}, {"dp": (z - 1) * CORES + core})

    def real(way, at):
        return at if way == 0 else nz - 1 - at

    def block_copy(way, chip):
        block = grads.at[chip * CORES + core]
        return remote(block, block, zsem.at[way, chip], zsem.at[2 + way, chip], ahead[way])

    def chain_copy(way, owner):
        block = chain.at[way, owner]
        return remote(block, block, zsem.at[4 + way, owner], zsem.at[6 + way, owner], ahead[way])

    def partner_copy(chip, side):
        block = grads.at[chip * CORES + side]
        return remote(block, block, zsem.at[8, chip], zsem.at[9, chip], partner)

    def cross_copy(chip):
        return remote(
            terms.at[chip * CORES + 1 - core], cross.at[chip], zsem.at[10, chip], zsem.at[11, chip], partner
        )

    def send_block(step):
        for way in (0, 1):
            @pl.when((spots[way] >= step) & (spots[way] < nz - 1))
            def _():
                block_copy(way, real(way, spots[way] - step)).start()

    send_block(0)
    partner_copy(z, core).start()

    up_t = jnp.transpose(up_f)
    for d in range(n_dp):
        upt[d] = up_t[d * depth : (d + 1) * depth].astype(BF16)

    def term(d):
        terms[d] = (fdot(upt[d], hidden[...]) * factor).astype(BF16)

    def other_terms(chip, carry):
        term(chip * CORES + 1 - core)
        cross_copy(chip).start()
        return carry

    def own_terms(chip, carry):
        term(chip * CORES + core)
        return carry

    lax.fori_loop(0, nz, other_terms, 0)
    lax.fori_loop(0, nz, own_terms, 0)

    def merge(chip, carry):
        cross_copy(chip).wait_recv()
        own = terms[chip * CORES + core].astype(F32)
        cross[chip] = (own + cross[chip].astype(F32)).astype(BF16)
        return carry

    lax.fori_loop(0, nz, merge, 0)

    for step in range(nz - 1):
        if step:
            send_block(step)
        for way in (0, 1):
            spot = spots[way]
            owner = real(way, nz - 1 + spot - step)

            @pl.when((spot <= step) & (spot == 0))
            def _():
                chain[way, owner] = cross[owner]
                chain_copy(way, owner).start()

            @pl.when((spot <= step) & (spot > 0))
            def _():
                chain_copy(way, owner).wait_recv()
                chain[way, owner] = (chain[way, owner].astype(F32) + cross[owner].astype(F32)).astype(BF16)
                chain_copy(way, owner).start()

        if step == min(1, nz - 2):
            near_sum()
        for way in (0, 1):
            @pl.when(spots[way] > step)
            def _():
                chip = real(way, spots[way] - 1 - step)
                block_copy(way, chip).wait_recv()
                partner_copy(chip, core).start()

    far_sum()

    for i in range(1, n_dp):
        to = (me_dp + i) % n_dp
        remote(nts.at[to], ntr.at[to], dsem.at[0, to], dsem.at[1, to], {"dp": to}).wait_recv()

    for chip in range(nz):
        partner_copy(chip, 1 - core).wait_recv()
    first = fdot(ntr[0], grads[0])
    for k in range(1, n_dp):
        first = first + fdot(ntr[k], grads[k])
    g1_o[...] = (first * factor).astype(BF16)

    for way in (0, 1):
        @pl.when(spots[way] > 0)
        def _():
            chain_copy(way, z).wait_recv()

        @pl.when(spots[way] == 0)
        def _():
            chain[way, z] = jnp.zeros_like(chain[way, z])

    second = cross[z].astype(F32) + chain[0, z].astype(F32) + chain[1, z].astype(F32)
    g2_o[...] = second.astype(BF16)

    tp_wait(u_block, urecv, 0, False)
    tp_wait(own_up, uall, 2, False)
    tp_wait(own_lin, linall, 4, False)
    early_sent()
    for i in range(1, n_dp):
        to = (me_dp + i) % n_dp
        remote(nts.at[to], ntr.at[to], dsem.at[0, to], dsem.at[1, to], {"dp": to}).wait_send()
    for chip in range(nz):
        partner_copy(chip, core).wait_send()
        cross_copy(chip).wait_send()
    for step in range(nz - 1):
        for way in (0, 1):
            spot = spots[way]

            @pl.when((spot >= step) & (spot < nz - 1))
            def _():
                block_copy(way, real(way, spot - step)).wait_send()

            @pl.when(spot <= step)
            def _():
                chain_copy(way, real(way, nz - 1 + spot - step)).wait_send()


def finish(early, first, second, early_o, first_o, second_o):
    early_o[...] = early[0 : early_o.shape[0], :]
    first_o[...] = first[...]
    second_o[...] = second[...]


def shards(partials, layer_input, ln_gain, ln_bias, fc1_weight, fc1_bias, fc2_weight, row_rank):
    n_tp = lax.axis_size("tp")
    n_dp = lax.axis_size("dp")
    nz = n_dp // CORES
    part = partials[0]
    rows, vis = part.shape
    slots, width = layer_input.shape
    hid = fc1_weight.shape[1]
    slot_pad = up_to(slots, 16)
    share = -(-rows // n_tp)
    share_pad = up_to(share, 16)
    depth = width // n_dp
    rest = vis - width
    outer = max(i for i in range(1, n_tp + 1) if n_tp % i == 0 and i * i <= n_tp)
    vmem = pl.BlockSpec(memory_space=pltpu.VMEM)
    anywhere = pl.BlockSpec(memory_space=pl.ANY)
    early, first, second = pl.pallas_call(
        functools.partial(kernel, n_tp, n_dp, outer, share, float(n_dp * rows) ** (-0.5)),
        out_shape=(
            jax.ShapeDtypeStruct((slot_pad, rest), BF16),
            jax.ShapeDtypeStruct((depth, hid), BF16),
            jax.ShapeDtypeStruct((depth, hid), BF16),
        ),
        in_specs=[vmem, anywhere, vmem, vmem, vmem, anywhere, vmem, anywhere],
        out_specs=(vmem, vmem, vmem),
        scratch_shapes=[
            pltpu.VMEM((rows, width), BF16),
            pltpu.VMEM((rows, rest), BF16),
            pltpu.VMEM((width, hid), BF16),
            pltpu.VMEM((width, hid), BF16),
            pltpu.VMEM((slot_pad, width), F32),
            pltpu.VMEM((slot_pad, width), BF16),
            pltpu.VMEM((n_tp, slot_pad, width), BF16),
            pltpu.VMEM((n_tp, share_pad, width), BF16),
            pltpu.VMEM((n_tp, share_pad, width), BF16),
            pltpu.VMEM((n_tp, share_pad, width), BF16),
            pltpu.VMEM((n_tp, slot_pad, rest), BF16),
            pltpu.VMEM((2, n_tp, slot_pad, rest // 2), BF16),
            pltpu.VMEM((2, n_tp // outer, slot_pad, rest // 2), BF16),
            pltpu.VMEM((rows, hid), BF16),
            pltpu.VMEM((rows, hid), F32),
            pltpu.VMEM((n_dp, depth, rows), BF16),
            pltpu.VMEM((n_dp, depth, rows), BF16),
            pltpu.VMEM((n_dp, depth, rows), BF16),
            pltpu.VMEM((n_dp, depth, hid), BF16),
            pltpu.VMEM((nz, depth, hid), BF16),
            pltpu.VMEM((2, nz, depth, hid), BF16),
            pltpu.VMEM((n_dp, rows, hid), BF16),
            pltpu.SemaphoreType.DMA((4,)),
            pltpu.SemaphoreType.DMA((6, n_tp)),
            pltpu.SemaphoreType.DMA((8, n_tp)),
            pltpu.SemaphoreType.DMA((2, n_dp)),
            pltpu.SemaphoreType.DMA((12, nz)),
        ],
        compiler_params=pltpu.CompilerParams(
            collective_id=0, has_side_effects=True, vmem_limit_bytes=58 * 1024 * 1024
        ),
        name="route_and_grads",
    )(
        row_rank.reshape(1, rows),
        part,
        layer_input,
        ln_gain,
        ln_bias,
        fc1_weight,
        fc1_bias,
        fc2_weight,
    )
    return pl.pallas_call(
        finish,
        out_shape=(
            jax.ShapeDtypeStruct((slots, rest), BF16),
            jax.ShapeDtypeStruct((depth, hid), BF16),
            jax.ShapeDtypeStruct((depth, hid), BF16),
        ),
        in_specs=[vmem, vmem, vmem],
        out_specs=(vmem, vmem, vmem),
        name="finish",
    )(early, first, second)


def solution(mesh):
    return jax.shard_map(
        shards,
        mesh=mesh,
        in_specs=(
            P("tp", "dp", None),
            P(("dp", "tp"), None),
            P(),
            P(),
            P(None, "tp"),
            P("tp"),
            P(None, "tp"),
            P("dp", None),
        ),
        out_specs=(P(("dp", "tp"), None), P("dp", "tp"), P("dp", "tp")),
        check_vma=False,
    )
```

```python
import functools

import jax
import jax.numpy as jnp
from jax import lax
from jax.experimental import pallas as pl
from jax.experimental.pallas import tpu as pltpu
from jax.sharding import PartitionSpec as P

MESH = pl.DeviceIdType.MESH
CORES = 2
F32 = jnp.float32
BF16 = jnp.bfloat16


def up_to(value, step):
    return -(-value // step) * step


def onehot(rows, columns, wanted, axis):
    at = lax.broadcasted_iota(jnp.int32, (rows, columns), axis).astype(F32)
    return jnp.where(at == wanted, 1.0, 0.0).astype(BF16)


def fdot(left, right):
    return jnp.dot(left, right, preferred_element_type=F32)


def kernel(
    n_tp, n_dp, outer, pieces, share, factor,
    rank_row, part, lin_own, gain, bias, fc1, b1, fc2,
    early_o, g1_o, g2_o,
    partu, parte, w1, w2, lin_wide, lin, linall, usend, urecv, uall, esend, near, far,
    hidden, deriv, nts, ntr, upt, terms, cross, chain, grads,
    lsem, tsem, esem, dsem, zsem,
):
    me_tp = lax.axis_index("tp")
    me_dp = lax.axis_index("dp")
    z, core = me_dp // CORES, me_dp % CORES
    nz = n_dp // CORES
    partner = {"dp": z * CORES + 1 - core}
    rows, width = partu.shape
    slot_pad = lin.shape[0]
    share_pad = usend.shape[1]
    hid = w1.shape[1]
    depth = g1_o.shape[0]
    step_h = 256 if hid % 256 == 0 else hid

    loads = [
        pltpu.make_async_copy(part.at[:, pl.ds(0, width)], partu, lsem.at[0]),
        pltpu.make_async_copy(part.at[:, pl.ds(width, parte.shape[1])], parte, lsem.at[1]),
        pltpu.make_async_copy(fc1, w1, lsem.at[2]),
        pltpu.make_async_copy(fc2, w2, lsem.at[3]),
    ]
    for load in loads:
        load.start()

    barrier = pltpu.get_barrier_semaphore()
    for i in range(1, n_tp):
        pl.semaphore_signal(barrier, inc=1, device_id={"tp": (me_tp + i) % n_tp}, device_id_type=MESH)
    for i in range(1, n_dp):
        pl.semaphore_signal(barrier, inc=1, device_id={"dp": (me_dp + i) % n_dp}, device_id_type=MESH)
    pl.semaphore_wait(barrier, n_tp + n_dp - 2)

    def remote(src, dst, send, recv, device):
        return pltpu.make_async_remote_copy(
            src_ref=src, dst_ref=dst, send_sem=send, recv_sem=recv, device_id=device, device_id_type=MESH
        )

    def tp_send(src_of, dst, kind):
        for i in range(1, n_tp):
            to = (me_tp + i) % n_tp
            remote(src_of(to), dst.at[me_tp], tsem.at[kind, to], tsem.at[kind + 1, me_tp], {"tp": to}).start()

    def tp_wait(src_of, dst, kind, recv):
        for i in range(1, n_tp):
            to = (me_tp + i) % n_tp
            copy = remote(src_of(to), dst.at[to], tsem.at[kind, to], tsem.at[kind + 1, to], {"tp": to})
            if recv:
                copy.wait_recv()
            else:
                copy.wait_send()

    slots = lin_own.shape[0]
    lin_wide[0:slots, :] = lin_own[...].astype(F32)
    if slot_pad > slots:
        lin_wide[slots:slot_pad, :] = jnp.zeros((slot_pad - slots, width), F32)
    lin[...] = lin_wide[...].astype(BF16)

    own_lin = lambda to: lin
    u_block = lambda to: usend.at[to]
    own_up = lambda to: uall.at[me_tp]

    inner = n_tp // outer
    place_a, place_b = me_tp // inner, me_tp % inner
    half = esend.shape[2] // 2

    def axes(way):
        return ((place_b, inner), (place_a, outer)) if way == 0 else ((place_a, outer), (place_b, inner))

    def rank_of(way, first, second):
        return second * inner + first if way == 0 else first * inner + second

    def e_half(way, rank):
        return esend.at[rank, :, pl.ds(way * half, half)]

    def near_copy(way, i, other, sending):
        (first, extent), (second, count) = axes(way)
        peer = (first + i) % extent
        held = first if sending else peer
        return remote(
            e_half(way, rank_of(way, peer, other)),
            near.at[way, held * count + other],
            esem.at[way, peer * count + other],
            esem.at[2 + way, held * count + other],
            {"tp": rank_of(way, peer, second)},
        )

    def far_copy(way, i, sending):
        (first, extent), (second, count) = axes(way)
        peer = (second + i) % count
        held = second if sending else peer
        return remote(
            e_half(way, rank_of(way, first, peer)),
            far.at[way, held],
            esem.at[4 + way, peer],
            esem.at[6 + way, held],
            {"tp": rank_of(way, first, peer)},
        )

    def near_all(act):
        for other in range(n_tp):
            for way in (0, 1):
                (_, extent), (_, count) = axes(way)
                if other < count:
                    for i in range(1, extent):
                        act(near_copy(way, i, other, False))

    def near_start():
        for other in range(n_tp):
            for way in (0, 1):
                (_, extent), (_, count) = axes(way)
                if other < count:
                    for i in range(1, extent):
                        near_copy(way, i, other, True).start()

    def near_sum():
        near_all(lambda copy: copy.wait_recv())
        for way in (0, 1):
            (first, extent), (second, count) = axes(way)
            for i in list(range(1, count)) + [0]:
                other = (second + i) % count
                spot = rank_of(way, first, other)

                def add(c, carry):
                    columns = pl.ds(pl.multiple_of(c * chunk, 128), chunk)
                    mine = pl.ds(pl.multiple_of(way * half + c * chunk, 128), chunk)
                    block = esend[spot, :, mine].astype(F32)
                    for j in range(1, extent):
                        block = block + near[way, ((first + j) % extent) * count + other, :, columns].astype(F32)
                    esend[spot, :, mine] = block.astype(BF16)
                    return carry

                lax.fori_loop(0, half // chunk, add, 0)
                if i:
                    far_copy(way, i, True).start()

    def far_sum():
        for way in (0, 1):
            (first, extent), (second, count) = axes(way)
            for i in range(1, count):
                far_copy(way, i, False).wait_recv()

            def add(c, carry):
                columns = pl.ds(pl.multiple_of(c * chunk, 128), chunk)
                mine = pl.ds(pl.multiple_of(way * half + c * chunk, 128), chunk)
                block = esend[me_tp, :, mine].astype(F32)
                for j in range(1, count):
                    block = block + far[way, (second + j) % count, :, columns].astype(F32)
                early_o[:, mine] = block.astype(BF16)
                return carry

            lax.fori_loop(0, half // chunk, add, 0)

    def early_sent():
        near_all(lambda copy: copy.wait_send())
        for way in (0, 1):
            _, (_, count) = axes(way)
            for i in range(1, count):
                far_copy(way, i, False).wait_send()

    chunk = 640 if half % 640 == 0 else half

    r_row = lax.broadcasted_iota(jnp.int32, (1, rows), 1)
    r_col = lax.broadcasted_iota(jnp.int32, (rows, 1), 0)
    pad_row, pad_col = (r_row * 0).astype(F32), (r_col * 0).astype(F32)
    for i in range(1, n_tp):
        pad_row = pad_row + jnp.where(r_row >= i * share, 1.0, 0.0)
        pad_col = pad_col + jnp.where(r_col >= i * share, 1.0, 0.0)
    pad_row = r_row.astype(F32) + pad_row * (share_pad - share)
    pad_col = r_col.astype(F32) + pad_col * (share_pad - share)

    loads[0].wait()
    spread = onehot(n_tp * share_pad, rows, pad_row, 0)
    usend[...] = fdot(spread, partu[...]).astype(BF16).reshape(usend.shape)
    tp_send(u_block, urecv, 0)
    tp_send(own_lin, linall, 4)
    linall[me_tp] = lin[...]

    at0 = lax.broadcasted_iota(jnp.int32, (rows, rows), 0)
    at1 = lax.broadcasted_iota(jnp.int32, (rows, rows), 1)
    rank_r = rank_row[...].astype(F32)
    rank_c = jnp.sum(jnp.where(at0 == at1, rank_r, 0.0), axis=1, keepdims=True)
    same = rank_c == rank_r
    place_r = jnp.sum(jnp.where(same & (at0 < at1), 1.0, 0.0), axis=0, keepdims=True)
    place_c = jnp.sum(jnp.where(same & (at1 < at0), 1.0, 0.0), axis=1, keepdims=True)
    slot_r = rank_r * slot_pad + place_r
    slot_c = rank_c * slot_pad + place_c
    table = onehot(n_tp * slot_pad, rows, slot_r, 0)
    back = onehot(rows, n_tp * slot_pad, slot_c, 1)

    loads[1].wait()

    def place(i, carry):
        columns = pl.ds(pl.multiple_of(i * width, 128), width)
        placed = fdot(table, parte[:, columns]).astype(BF16)
        esend[:, :, columns] = placed.reshape(n_tp, slot_pad, width)
        return carry

    lax.fori_loop(0, parte.shape[1] // width, place, 0)

    tp_wait(u_block, urecv, 0, True)
    total = usend[me_tp].astype(F32)
    for i in range(1, n_tp):
        total = total + urecv[(me_tp + i) % n_tp].astype(F32)
    uall[me_tp] = total.astype(BF16)
    tp_send(own_up, uall, 2)
    near_start()

    tp_wait(own_lin, linall, 4, True)
    values = fdot(back, linall[...].reshape(n_tp * slot_pad, width))
    centered = values - jnp.mean(values, axis=1, keepdims=True)
    variance = jnp.mean(centered * centered, axis=1, keepdims=True)
    normed = centered / jnp.sqrt(variance + 1e-05) * gain[...].reshape(1, width) + bias[...].reshape(1, width)
    normed_t = jnp.transpose(normed)
    for d in range(n_dp):
        nts[d] = normed_t[d * depth : (d + 1) * depth].astype(BF16)
    normed = normed.astype(BF16)
    for i in range(1, n_dp):
        to = (me_dp + i) % n_dp
        remote(nts.at[to], ntr.at[me_dp], dsem.at[0, to], dsem.at[1, me_dp], {"dp": to}).start()
    ntr[me_dp] = nts[me_dp]

    loads[2].wait()

    def forward(i, carry):
        columns = pl.ds(pl.multiple_of(i * step_h, step_h), step_h) if step_h != hid else slice(None)
        preact = fdot(normed, w1[:, columns]) + b1[columns].reshape(1, step_h)
        cdf = 0.5 * (1.0 + lax.erf(preact * 0.7071067811865476))
        density = jnp.exp(-0.5 * preact * preact) * 0.3989422804014327
        hidden[:, columns] = (preact * cdf).astype(BF16)
        deriv[:, columns] = cdf + preact * density
        return carry

    lax.fori_loop(0, hid // step_h, forward, 0)

    loads[3].wait()
    tp_wait(own_up, uall, 2, True)
    gather = onehot(rows, n_tp * share_pad, pad_col, 1)
    up_f = fdot(gather, uall[...].reshape(n_tp * share_pad, width))
    up = up_f.astype(BF16)

    def backward(i, carry):
        columns = pl.ds(pl.multiple_of(i * step_h, step_h), step_h) if step_h != hid else slice(None)
        grads[me_dp, :, columns] = (fdot(up, w2[:, columns]) * deriv[:, columns]).astype(BF16)
        return carry

    lax.fori_loop(0, hid // step_h, backward, 0)

    spots = (z, nz - 1 - z)
    ahead = ({"dp": (z + 1) * CORES + core}, {"dp": (z - 1) * CORES + core})

    def real(way, at):
        return at if way == 0 else nz - 1 - at

    def part_of(extent, piece):
        return pl.ds(piece * (extent // pieces), extent // pieces)

    def block_copy(way, chip, piece):
        block = grads.at[chip * CORES + core, part_of(rows, piece)]
        at = chip * pieces + piece
        return remote(block, block, zsem.at[way, at], zsem.at[2 + way, at], ahead[way])

    def chain_copy(way, owner, piece):
        block = chain.at[way, owner, part_of(depth, piece)]
        at = owner * pieces + piece
        return remote(block, block, zsem.at[4 + way, at], zsem.at[6 + way, at], ahead[way])

    def partner_copy(chip, side):
        block = grads.at[chip * CORES + side]
        return remote(block, block, zsem.at[8, chip], zsem.at[9, chip], partner)

    def cross_copy(chip):
        return remote(
            terms.at[chip * CORES + 1 - core], cross.at[chip], zsem.at[10, chip], zsem.at[11, chip], partner
        )

    for piece in range(pieces):
        for way in (0, 1):
            @pl.when(spots[way] < nz - 1)
            def _():
                block_copy(way, z, piece).start()

    up_t = jnp.transpose(up_f)
    for d in range(n_dp):
        upt[d] = up_t[d * depth : (d + 1) * depth].astype(BF16)

    def term(d):
        terms[d] = (fdot(upt[d], hidden[...]) * factor).astype(BF16)

    def other_terms(chip, carry):
        term(chip * CORES + 1 - core)
        cross_copy(chip).start()
        return carry

    def own_terms(chip, carry):
        term(chip * CORES + core)
        return carry

    lax.fori_loop(0, nz, other_terms, 0)
    partner_copy(z, core).start()
    lax.fori_loop(0, nz, own_terms, 0)

    def merge(chip, carry):
        cross_copy(chip).wait_recv()
        own = terms[chip * CORES + core].astype(F32)
        cross[chip] = (own + cross[chip].astype(F32)).astype(BF16)
        return carry

    lax.fori_loop(0, nz, merge, 0)

    for step in range(nz - 1):
        for piece in range(pieces):
            part_rows = part_of(depth, piece)
            for way in (0, 1):
                spot = spots[way]
                owner = real(way, nz - 1 + spot - step)

                @pl.when((spot <= step) & (spot == 0))
                def _():
                    chain[way, owner, part_rows] = cross[owner, part_rows]
                    chain_copy(way, owner, piece).start()

                @pl.when((spot <= step) & (spot > 0))
                def _():
                    chain_copy(way, owner, piece).wait_recv()
                    chain[way, owner, part_rows] = (
                        chain[way, owner, part_rows].astype(F32) + cross[owner, part_rows].astype(F32)
                    ).astype(BF16)
                    chain_copy(way, owner, piece).start()

            for way in (0, 1):
                chip = real(way, spots[way] - 1 - step)

                @pl.when(spots[way] > step)
                def _():
                    block_copy(way, chip, piece).wait_recv()

                @pl.when((spots[way] > step) & (spots[way] < nz - 1))
                def _():
                    block_copy(way, chip, piece).start()

            if piece == pieces - 1:
                for way in (0, 1):
                    @pl.when(spots[way] > step)
                    def _():
                        partner_copy(real(way, spots[way] - 1 - step), core).start()

        if step == 0:
            near_sum()

    far_sum()

    for i in range(1, n_dp):
        to = (me_dp + i) % n_dp
        remote(nts.at[to], ntr.at[to], dsem.at[0, to], dsem.at[1, to], {"dp": to}).wait_recv()

    for chip in range(nz):
        partner_copy(chip, 1 - core).wait_recv()
    first = fdot(ntr[0], grads[0])
    for k in range(1, n_dp):
        first = first + fdot(ntr[k], grads[k])
    g1_o[...] = (first * factor).astype(BF16)

    for way in (0, 1):
        @pl.when(spots[way] > 0)
        def _():
            for piece in range(pieces):
                chain_copy(way, z, piece).wait_recv()

        @pl.when(spots[way] == 0)
        def _():
            chain[way, z] = jnp.zeros_like(chain[way, z])

    second = cross[z].astype(F32) + chain[0, z].astype(F32) + chain[1, z].astype(F32)
    g2_o[...] = second.astype(BF16)

    tp_wait(u_block, urecv, 0, False)
    tp_wait(own_up, uall, 2, False)
    tp_wait(own_lin, linall, 4, False)
    early_sent()
    for i in range(1, n_dp):
        to = (me_dp + i) % n_dp
        remote(nts.at[to], ntr.at[to], dsem.at[0, to], dsem.at[1, to], {"dp": to}).wait_send()
    for chip in range(nz):
        partner_copy(chip, core).wait_send()
        cross_copy(chip).wait_send()
    for step in range(nz - 1):
        for piece in range(pieces):
            for way in (0, 1):
                spot = spots[way]

                @pl.when((spot >= step) & (spot < nz - 1))
                def _():
                    block_copy(way, real(way, spot - step), piece).wait_send()

                @pl.when(spot <= step)
                def _():
                    chain_copy(way, real(way, nz - 1 + spot - step), piece).wait_send()


def finish(early, first, second, early_o, first_o, second_o):
    early_o[...] = early[0 : early_o.shape[0], :]
    first_o[...] = first[...]
    second_o[...] = second[...]


def shards(partials, layer_input, ln_gain, ln_bias, fc1_weight, fc1_bias, fc2_weight, row_rank):
    n_tp = lax.axis_size("tp")
    n_dp = lax.axis_size("dp")
    nz = n_dp // CORES
    part = partials[0]
    rows, vis = part.shape
    slots, width = layer_input.shape
    hid = fc1_weight.shape[1]
    slot_pad = up_to(slots, 16)
    share = -(-rows // n_tp)
    share_pad = up_to(share, 16)
    depth = width // n_dp
    rest = vis - width
    pieces = 2 if depth % 32 == 0 and rows % 32 == 0 else 1
    outer = max(i for i in range(1, n_tp + 1) if n_tp % i == 0 and i * i <= n_tp)
    vmem = pl.BlockSpec(memory_space=pltpu.VMEM)
    anywhere = pl.BlockSpec(memory_space=pl.ANY)
    early, first, second = pl.pallas_call(
        functools.partial(kernel, n_tp, n_dp, outer, pieces, share, float(n_dp * rows) ** (-0.5)),
        out_shape=(
            jax.ShapeDtypeStruct((slot_pad, rest), BF16),
            jax.ShapeDtypeStruct((depth, hid), BF16),
            jax.ShapeDtypeStruct((depth, hid), BF16),
        ),
        in_specs=[vmem, anywhere, vmem, vmem, vmem, anywhere, vmem, anywhere],
        out_specs=(vmem, vmem, vmem),
        scratch_shapes=[
            pltpu.VMEM((rows, width), BF16),
            pltpu.VMEM((rows, rest), BF16),
            pltpu.VMEM((width, hid), BF16),
            pltpu.VMEM((width, hid), BF16),
            pltpu.VMEM((slot_pad, width), F32),
            pltpu.VMEM((slot_pad, width), BF16),
            pltpu.VMEM((n_tp, slot_pad, width), BF16),
            pltpu.VMEM((n_tp, share_pad, width), BF16),
            pltpu.VMEM((n_tp, share_pad, width), BF16),
            pltpu.VMEM((n_tp, share_pad, width), BF16),
            pltpu.VMEM((n_tp, slot_pad, rest), BF16),
            pltpu.VMEM((2, n_tp, slot_pad, rest // 2), BF16),
            pltpu.VMEM((2, n_tp // outer, slot_pad, rest // 2), BF16),
            pltpu.VMEM((rows, hid), BF16),
            pltpu.VMEM((rows, hid), F32),
            pltpu.VMEM((n_dp, depth, rows), BF16),
            pltpu.VMEM((n_dp, depth, rows), BF16),
            pltpu.VMEM((n_dp, depth, rows), BF16),
            pltpu.VMEM((n_dp, depth, hid), BF16),
            pltpu.VMEM((nz, depth, hid), BF16),
            pltpu.VMEM((2, nz, depth, hid), BF16),
            pltpu.VMEM((n_dp, rows, hid), BF16),
            pltpu.SemaphoreType.DMA((4,)),
            pltpu.SemaphoreType.DMA((6, n_tp)),
            pltpu.SemaphoreType.DMA((8, n_tp)),
            pltpu.SemaphoreType.DMA((2, n_dp)),
            pltpu.SemaphoreType.DMA((12, nz * pieces)),
        ],
        compiler_params=pltpu.CompilerParams(
            collective_id=0, has_side_effects=True, vmem_limit_bytes=58 * 1024 * 1024
        ),
        name="route_and_grads",
    )(
        row_rank.reshape(1, rows),
        part,
        layer_input,
        ln_gain,
        ln_bias,
        fc1_weight,
        fc1_bias,
        fc2_weight,
    )
    return pl.pallas_call(
        finish,
        out_shape=(
            jax.ShapeDtypeStruct((slots, rest), BF16),
            jax.ShapeDtypeStruct((depth, hid), BF16),
            jax.ShapeDtypeStruct((depth, hid), BF16),
        ),
        in_specs=[vmem, vmem, vmem],
        out_specs=(vmem, vmem, vmem),
        name="finish",
    )(early, first, second)


def solution(mesh):
    return jax.shard_map(
        shards,
        mesh=mesh,
        in_specs=(
            P("tp", "dp", None),
            P(("dp", "tp"), None),
            P(),
            P(),
            P(None, "tp"),
            P("tp"),
            P(None, "tp"),
            P("dp", None),
        ),
        out_specs=(P(("dp", "tp"), None), P("dp", "tp"), P("dp", "tp")),
        check_vma=False,
    )
```
